256 devices in a mesh: dp: 32 (over x, y, core), tp: 8 (over z).
Axes of the slice: x: 4, y: 4, z: 8, core: 2. Of those that a mesh axis runs over, the one named last changes fastest.
Arguments:
- arrived_rows: bfloat16 [12288, 7168], P('dp', 'tp'), may hold values from -6 to 6
- row_counts: int32 [32], P('dp'), may hold values from 1 to 384, 4096 in all
- routes: int32 [4096, 8], P('dp'), may hold values from 0 to 31, all different within a row; in each aligned block of 128 rows (0 to 127, 128 to 255, ...) at most 40 rows name the same one
- gate_scale: float32 [4096, 8], P('dp'), may hold values from 0.1 to 0.6
- w_gate: bfloat16 [32, 7168, 1024], P('dp', 'tp'), may hold values from -0.0625 to 0.0625
- w_up: bfloat16 [32, 7168, 1024], P('dp', 'tp'), may hold values from -0.0625 to 0.0625
- w_down: bfloat16 [32, 1024, 7168], P('dp', None, 'tp'), may hold values from -0.1875 to 0.1875
- cotangent: bfloat16 [4096, 7168], P('dp', 'tp'), may hold values from -6 to 6
Outputs:
- layer_out: bfloat16 [4096, 7168], P('dp', 'tp')
- grad_rows: bfloat16 [12288, 7168], P('dp', 'tp')
The draws below stay inside these ranges and needn't reach their ends.
Inputs may be any that keep to these rules, and one draw needn't show every extreme that they name: `row_counts`: the counts sum to exactly 4096; the largest is exactly 384. `routes`: each row names 8 different experts; within the 128 rows of one index of dp no expert is named by more than 40 rows, a bound that some block reaches.
All inputs are finite; a program needn't handle non-finite values. No bound on the sum of `row_counts` on one device may be relied on, other than what follows from the above.
Results may differ from the reference program's by a relative error of at most 0.03.
Values may be sent and summed in bfloat16 or wider, within the bound.
No kernel may reach another device: no remote copies, remote signals or barrier semaphores. Data moves between devices by JAX's collectives and lax.ppermute only.
A program may use at most 64 MiB of HBM per device.

```python
import math
import jax
import jax.numpy as jnp
import numpy as np
from jax import lax

D = 7168
FF = 1024
ROWS = 128
D_PART = 896
SLOTS = 384
ACCEPT = 4096
EXPERTS = 32
TOPK = 8
CAP = 40
N_DP = 32
N_TP = 8


def levels(key, shape, cuts, smallest, largest):
    factor_of, own = 1.0, jax.random.fold_in(key, 6)
    for position, parts in cuts:
        draws = jnp.exp(jax.random.uniform(jax.random.fold_in(own, position), (parts,), jnp.float32, smallest / len(cuts), largest / len(cuts)))
        factor_of = factor_of * jnp.repeat(draws, shape[position] // parts).reshape([-1 if axis == position else 1 for axis in range(len(shape))])
    return factor_of


def split_up(amount, total, reach, lean):
    weights = [(1 << 20) // math.isqrt(standing ** lean) + 1 for standing in range(2, amount + 1)]
    spare, holding = total - reach - (amount - 1), [1] * (amount - 1)
    while spare > 0:
        free = [i for i in range(amount - 1) if holding[i] < reach]
        whole, remaining = sum([weights[i] for i in free]), spare
        for i in free:
            extra = min(reach - holding[i], max(1, remaining * weights[i] // whole), spare)
            holding[i] = holding[i] + extra
            spare = spare - extra
    return np.array([reach] + holding)


def ragged_sizes(own_key, amount, total, bound, lean):
    if amount == 2:
        one = jax.random.randint(own_key, (), max(1, total - bound), min(bound, total - 1) + 1)
        return jnp.stack([one, total - one])
    tallies = jnp.asarray(split_up(amount, total, bound, lean), jnp.int32)
    twos = (amount - 1) // 2
    source_of, taker = tallies[1:1 + 2 * twos:2], tallies[2:2 + 2 * twos:2]
    slack = jnp.minimum(source_of - 1, bound - taker)
    shifted = jax.random.randint(jax.random.fold_in(own_key, 1), (twos,), 0, 1 << 20) % (slack + 1)
    tallies = tallies.at[1:1 + 2 * twos:2].set(source_of - shifted).at[2:2 + 2 * twos:2].set(taker + shifted)
    return tallies[jax.random.permutation(jax.random.fold_in(own_key, 2), amount)]


def routed_block(own_key, own, number, rows, number_of, top, reach, slope):
    order = jax.random.permutation(own_key, number_of)
    heavy_load, common = portions_of(number_of, rows * top, reach, slope, True), portions_of(number_of, rows * top, reach, slope, False)
    places = jnp.arange(number_of)

    def named(tallies, turn):
        used = int((tallies > 0).sum())
        fixed = max(1, used // 4)
        moved = fixed + (places - fixed + turn * (used - fixed)) % max(1, number_of - fixed)
        return jnp.zeros((number_of,), jnp.int32).at[order[jnp.where(places < fixed, places, moved)]].set(jnp.asarray(tallies, jnp.int32))

    tallies = jnp.where(number % 4 == 0, named(heavy_load, number // 4), named(common, number - number // 4 - 1))
    mixed = jax.random.permutation(jax.random.fold_in(own, 3), number_of)
    donor, sink = mixed[0:number_of // 2 * 2:2], mixed[1:number_of // 2 * 2:2]
    slack = jnp.minimum(tallies[donor] - 1, reach - tallies[sink]) // 2
    slack = jnp.where((donor == order[0]) | (sink == order[0]) | (tallies[sink] == 0), 0, jnp.maximum(slack, 0))
    moved = jax.random.randint(jax.random.fold_in(own, 4), (number_of // 2,), 0, 1 << 20) % (slack + 1)
    tallies = tallies.at[donor].add(-moved).at[sink].add(moved)
    items = jnp.searchsorted(jnp.cumsum(tallies), jnp.arange(rows * top), side="right").astype(jnp.int32)
    listing = items.reshape(top, rows).T
    listing = listing[jax.random.permutation(jax.random.fold_in(own, 1), rows)]
    turn = jax.random.randint(jax.random.fold_in(own, 2), (rows, 1), 0, top)
    return jnp.take_along_axis(listing, (jnp.arange(top)[None, :] + turn) % top, axis=1)


def portions_of(count, total, bound, lean, full):
    weights = [(1 << 20) // math.isqrt(grade ** lean) + 1 for grade in range(1, count + 1)]
    largest = bound if full else min(bound, max(-(-total // count), total * weights[0] // sum(weights)))
    least = 1 if total - largest >= count - 1 else 0
    given, spare = [largest] + [least] * (count - 1), total - largest - least * (count - 1)
    while spare > 0:
        free = [i for i in range(1, count) if given[i] < largest] or [i for i in range(1, count) if given[i] < bound]
        whole, left = sum([weights[i] for i in free]), spare
        for i in free:
            more = min(bound - given[i], max(1, left * weights[i] // whole), spare)
            given[i] = given[i] + more
            spare = spare - more
    return np.array(given)


def scatter_about(stream_key, extent, scale, limit, pieces=(), kind=jnp.bfloat16):
    values = scale * jax.random.normal(stream_key, extent, jnp.float32)
    if pieces:
        values = values * levels(stream_key, extent, pieces, -0.22, 0.18)
    return jnp.clip(values, -limit, limit).astype(kind)


def setup_inputs(seed: int = 0) -> dict:
    splits = jax.random.split(jax.random.key(seed), 9)
    arrived_rows = scatter_about(splits[0], (N_DP * SLOTS, D), 1.0, 6.0, ((0, 32), (1, 8)))
    row_counts = ragged_sizes(splits[1], N_DP, ACCEPT, SLOTS, 2).astype(jnp.int32)
    routes_keys = jax.random.split(jax.random.fold_in(splits[2], 1), ACCEPT // ROWS)
    routes_turns = jax.random.permutation(jax.random.fold_in(splits[2], 3), ACCEPT // ROWS)
    routes = jax.vmap(lambda own, number: routed_block(jax.random.fold_in(splits[2], 2), own, number, ROWS, EXPERTS, TOPK, CAP, 0))(routes_keys, routes_turns).reshape((ACCEPT, TOPK))
    gate_scale = jnp.clip(0.1 + 0.5 * jax.random.uniform(splits[3], (ACCEPT, TOPK), jnp.float32) ** levels(splits[3], (ACCEPT, TOPK), ((0, 32),), -0.2, 0.2), 0.1, 0.6)
    w_gate = scatter_about(splits[4], (EXPERTS, D, FF), D ** -0.5, 0.0625, ((0, 32), (1, 8)))
    w_up = scatter_about(splits[5], (EXPERTS, D, FF), D ** -0.5, 0.0625, ((0, 32), (1, 8)))
    w_down = scatter_about(splits[6], (EXPERTS, FF, D), FF ** -0.5, 0.1875, ((0, 32), (2, 8)))
    cotangent = scatter_about(splits[7], (ACCEPT, D), 1.0, 6.0, ((0, 32), (1, 8)))
    return {"arrived_rows": arrived_rows, "row_counts": row_counts, "routes": routes, "gate_scale": gate_scale, "w_gate": w_gate, "w_up": w_up, "w_down": w_down, "cotangent": cotangent}


def block_sum(left, right, pattern):
    partial_value = jnp.einsum(pattern, left.astype(jnp.float32), right.astype(jnp.float32))
    rounded = lax.optimization_barrier(partial_value.astype(jnp.bfloat16))
    return jnp.sum(rounded.astype(jnp.float32), axis=1)


def reference(arrived_rows, row_counts, routes, gate_scale, w_gate, w_up, w_down, cotangent):
    counts = row_counts.astype(jnp.int32)
    starts = (jnp.cumsum(counts) - counts).astype(jnp.int32)
    global_rank = (jnp.arange(ROWS, dtype=jnp.int32)[None, :] * EXPERTS + jnp.arange(EXPERTS, dtype=jnp.int32)[:, None]).reshape(-1)
    source = (jnp.sum((starts[None, :] <= global_rank[:, None]).astype(jnp.int32), axis=1) - 1).astype(jnp.int32)
    arrival_index = (source * SLOTS + global_rank - starts[source]).astype(jnp.int32)
    balanced = arrived_rows[arrival_index]
    expert_ids = routes.reshape(-1).astype(jnp.int32)
    pair_total = ACCEPT * TOPK
    ordering = jnp.argsort(expert_ids, stable=True).astype(jnp.int32)
    expert_load = jnp.sum((expert_ids[:, None] == jnp.arange(EXPERTS, dtype=jnp.int32)[None, :]).astype(jnp.int32), axis=0)
    offsets = (jnp.cumsum(expert_load) - expert_load).astype(jnp.int32)
    window = EXPERTS * CAP
    flat_scale = gate_scale.reshape(-1)

    def per_expert(totals, expert):
        out_total, grad_total = totals
        slots = jnp.arange(window, dtype=jnp.int32)
        positions = jnp.clip(offsets[expert] + slots, 0, pair_total - 1).astype(jnp.int32)
        chosen = ordering[positions]
        token_row = (chosen // TOPK).astype(jnp.int32)
        scales = jnp.where(slots < expert_load[expert], flat_scale[chosen], jnp.zeros((), jnp.float32))
        inputs = balanced[token_row].reshape(window, N_TP, D_PART)
        grads_in = cotangent[token_row].reshape(window, N_TP, D_PART)
        gate_w = w_gate[expert].reshape(N_TP, D_PART, FF)
        up_w = w_up[expert].reshape(N_TP, D_PART, FF)
        down_w = w_down[expert]
        gate_pre = block_sum(inputs, gate_w, "wbd,bdf->wbf")
        up_pre = block_sum(inputs, up_w, "wbd,bdf->wbf")
        hidden = (jax.nn.silu(gate_pre) * up_pre).astype(jnp.bfloat16)
        expert_out = jnp.dot(hidden, down_w, preferred_element_type=jnp.float32).astype(jnp.bfloat16)
        hidden_grad = block_sum(grads_in, down_w.reshape(FF, N_TP, D_PART), "wbd,fbd->wbf")
        sigmoid_gate = jax.nn.sigmoid(gate_pre)
        gate_grad = (hidden_grad * up_pre * sigmoid_gate * (1.0 + gate_pre * (1.0 - sigmoid_gate))).astype(jnp.bfloat16)
        up_grad = (hidden_grad * gate_pre * sigmoid_gate).astype(jnp.bfloat16)
        input_grad = (jnp.dot(gate_grad, w_gate[expert].T, preferred_element_type=jnp.float32)
                      + jnp.dot(up_grad, w_up[expert].T, preferred_element_type=jnp.float32)).astype(jnp.bfloat16)
        out_total = out_total.at[token_row].add(scales[:, None] * expert_out.astype(jnp.float32))
        grad_total = grad_total.at[token_row].add(scales[:, None] * input_grad.astype(jnp.float32))
        return (out_total, grad_total), None

    zeros_out = jnp.zeros((ACCEPT, D), jnp.float32)
    (out_total, grad_total), _ = lax.scan(per_expert, (zeros_out, zeros_out), jnp.arange(EXPERTS, dtype=jnp.int32))
    layer_out = out_total.astype(jnp.bfloat16)
    balanced_grad = grad_total.astype(jnp.bfloat16)
    slot_ids = jnp.arange(SLOTS, dtype=jnp.int32)[None, :]
    arrival_rank = starts[:, None] + slot_ids
    usable = slot_ids < counts[:, None]
    back_pos = jnp.clip((arrival_rank % EXPERTS) * ROWS + arrival_rank // EXPERTS, 0, ACCEPT - 1).astype(jnp.int32)
    grad_rows = jnp.where(usable[:, :, None], balanced_grad[back_pos], jnp.zeros((), jnp.bfloat16))
    return layer_out, grad_rows.reshape(EXPERTS * SLOTS, D)
```

```python
import jax
import jax.numpy as jnp
from jax import lax
from jax.sharding import PartitionSpec as P

BF = jnp.bfloat16
F32 = jnp.float32


def rounded(tensor):
    return lax.optimization_barrier(tensor.astype(BF))


def select(left, right):
    return jnp.dot(left, right, preferred_element_type=F32).astype(BF)


def select_t(left, right):
    return lax.dot_general(
        left, right, (((0,), (0,)), ((), ())), preferred_element_type=F32
    ).astype(BF)


def dot_nt(left, right):
    return lax.dot_general(left, right, (((1,), (1,)), ((), ())), preferred_element_type=F32)


def on_device(arrived_rows, row_counts, routes, gate_scale, w_gate, w_up, w_down, cotangent):
    members = lax.axis_size("dp")
    myself = lax.axis_index("dp")
    slot_count, part = arrived_rows.shape
    rows, top = routes.shape
    capacity = rows * top // members + rows * top // (4 * members)
    per_peer = -(-(slot_count // members) // 16) * 16
    gate_proj, up_proj, down_proj = w_gate[0], w_up[0], w_down[0]

    def exchange(tensor):
        return lax.all_to_all(tensor, "dp", split_axis=0, concat_axis=0, tiled=True)

    ids = jnp.arange(members, dtype=jnp.int32)
    chosen = routes.T[None, :, :] == ids[:, None, None]
    named = jnp.any(chosen, axis=1)
    before = jnp.arange(rows)[:, None] < jnp.arange(rows)[None, :]
    place = jnp.dot(named.astype(BF), before.astype(BF), preferred_element_type=F32)
    place = jnp.where(named, place.astype(jnp.int32), -1)
    slots = jnp.arange(capacity, dtype=jnp.int32)
    hot = place[:, None, :] == slots[None, :, None]
    pack = hot.astype(BF).reshape(members * capacity, rows)
    shipped_grad = exchange(select(pack, cotangent).reshape(members, capacity, part))

    all_counts = lax.all_gather(row_counts, "dp", axis=0, tiled=True)
    starts = jnp.sum(jnp.where(ids[None, :] < ids[:, None], all_counts[None, :], 0), axis=1)
    my_start = starts[myself]
    my_count = all_counts[myself]
    column = jnp.arange(per_peer, dtype=jnp.int32)
    source_slot = (ids[:, None] - my_start) % members + column[None, :] * members
    source_slot = jnp.where(source_slot < my_count, source_slot, -1).reshape(-1)
    spread = (source_slot[:, None] == jnp.arange(slot_count, dtype=jnp.int32)[None, :]).astype(BF)
    incoming = exchange(select(spread, arrived_rows).reshape(members, per_peer, part))
    offset = (jnp.arange(rows, dtype=jnp.int32) * members + myself)[:, None] - starts[None, :]
    held = (offset >= 0) & (offset < all_counts[None, :])
    taken = jnp.where(held, offset // members, -1)
    take = (taken[:, :, None] == column[None, None, :]).astype(BF).reshape(rows, -1)
    balanced = select(take, incoming.reshape(-1, part))
    shipped = exchange(select(pack, balanced).reshape(members, capacity, part))

    grad_part = rounded(dot_nt(shipped_grad.reshape(-1, part), down_proj))
    hidden_grad = lax.psum_scatter(grad_part, "tp", scatter_dimension=0, tiled=True)

    flat = shipped.reshape(-1, part)
    gate_part = rounded(jnp.dot(flat, gate_proj, preferred_element_type=F32))
    up_part = rounded(jnp.dot(flat, up_proj, preferred_element_type=F32))
    gate_pre = lax.psum_scatter(gate_part, "tp", scatter_dimension=0, tiled=True)
    up_pre = lax.psum_scatter(up_part, "tp", scatter_dimension=0, tiled=True)
    gate_pre, up_pre, hidden_grad = (v.astype(F32) for v in (gate_pre, up_pre, hidden_grad))
    sigmoid_gate = jax.nn.sigmoid(gate_pre)
    hidden = (gate_pre * sigmoid_gate * up_pre).astype(BF)
    gate_grad = (
        hidden_grad * up_pre * sigmoid_gate * (1.0 + gate_pre * (1.0 - sigmoid_gate))
    ).astype(BF)
    up_grad = (hidden_grad * gate_pre * sigmoid_gate).astype(BF)
    gate_grad = lax.all_gather(gate_grad, "tp", axis=0, tiled=True)
    up_grad = lax.all_gather(up_grad, "tp", axis=0, tiled=True)
    hidden = lax.all_gather(hidden, "tp", axis=0, tiled=True)

    scale_high = lax.optimization_barrier(gate_scale.astype(BF))
    scale_low = (gate_scale - scale_high.astype(F32)).astype(BF)

    def weights(scale):
        per_expert = jnp.sum(jnp.where(chosen, scale.astype(F32).T[None], 0.0), axis=1)
        return jnp.where(hot, per_expert[:, None, :], 0.0).astype(BF).reshape(-1, rows)

    mix = jnp.concatenate([weights(scale_high), weights(scale_low)], axis=1)

    def combine(returned):
        both = lax.dot_general(
            mix, returned.reshape(-1, part), (((0,), (0,)), ((), ())), preferred_element_type=F32
        )
        return (both[:rows] + both[rows:]).astype(BF)

    input_grad = (dot_nt(gate_grad, gate_proj) + dot_nt(up_grad, up_proj)).astype(BF)
    returned_grad = exchange(input_grad.reshape(members, capacity, part))
    expert_out = jnp.dot(hidden, down_proj, preferred_element_type=F32).astype(BF)
    returned_out = exchange(expert_out.reshape(members, capacity, part))
    balanced_grad = combine(returned_grad)
    leaving = select_t(take, balanced_grad)
    arriving = exchange(leaving.reshape(members, per_peer, part))
    grad_rows = select_t(spread, arriving.reshape(-1, part))
    layer_out = combine(returned_out)
    return (layer_out, grad_rows)


def solution(mesh):
    placed = (
        P("dp", "tp"),
        P("dp"),
        P("dp", None),
        P("dp", None),
        P("dp", "tp", None),
        P("dp", "tp", None),
        P("dp", None, "tp"),
        P("dp", "tp"),
    )
    return jax.shard_map(
        on_device,
        mesh=mesh,
        in_specs=placed,
        out_specs=(P("dp", "tp"), P("dp", "tp")),
        check_vma=False,
    )
```

```python
import jax
import jax.numpy as jnp
from jax import lax
from jax.sharding import PartitionSpec as P

BF = jnp.bfloat16
F32 = jnp.float32


def rounded(tensor):
    return lax.optimization_barrier(tensor.astype(BF))


def select(left, right):
    return jnp.dot(left, right, preferred_element_type=F32).astype(BF)


def select_t(left, right):
    return lax.dot_general(
        left, right, (((0,), (0,)), ((), ())), preferred_element_type=F32
    ).astype(BF)


def dot_nt(left, right):
    return lax.dot_general(left, right, (((1,), (1,)), ((), ())), preferred_element_type=F32)


def f32(tensor):
    return tensor.astype(F32)


def ring_steps():
    size = lax.axis_size("tp")
    up = [(i, (i + 1) % size) for i in range(size)]
    down = [(i, (i - 1) % size) for i in range(size)]
    return (
        lambda t: lax.ppermute(t, "tp", up),
        lambda t: lax.ppermute(t, "tp", down),
        size,
    )


def ring_scatter(tensor):
    send_up, send_down, size = ring_steps()
    me = lax.axis_index("tp")
    half = tensor.shape[2] // 2

    def own(k):
        return lax.dynamic_index_in_dim(tensor, k % size, 0, keepdims=False)

    far = own(me + size // 2)
    a, b = send_up(far[:, :half]), send_down(far[:, half:])
    for s in range(size // 2 - 1, 0, -1):
        own_a, own_b = own(me + s), own(me - s)
        if s == size // 2 - 1:
            a = jnp.concatenate([(f32(a) + f32(own_a[:, :half])).astype(BF), own_a[:, half:]], 1)
            b = jnp.concatenate([own_b[:, :half], (f32(b) + f32(own_b[:, half:])).astype(BF)], 1)
        else:
            a = (f32(a) + f32(own_a)).astype(BF)
            b = (f32(b) + f32(own_b)).astype(BF)
        a, b = send_up(a), send_down(b)
    return f32(own(me)) + f32(a) + f32(b)


def ring_gather(shard):
    send_up, send_down, size = ring_steps()
    me = lax.axis_index("tp")
    half = shard.shape[1] // 2
    whole = jnp.zeros((size,) + shard.shape, shard.dtype)

    def put(whole, piece, k):
        return lax.dynamic_update_slice(whole, piece[None], (k % size, 0, 0))

    whole = put(whole, shard, me)
    a = b = shard
    for s in range(1, size // 2):
        a, b = send_up(a), send_down(b)
        whole = put(put(whole, a, me - s), b, me + s)
    a, b = send_up(a[:, :half]), send_down(b[:, half:])
    return put(whole, jnp.concatenate([a, b], 1), me + size // 2)


def on_device(arrived_rows, row_counts, routes, gate_scale, w_gate, w_up, w_down, cotangent):
    members = lax.axis_size("dp")
    myself = lax.axis_index("dp")
    slot_count, part = arrived_rows.shape
    rows, top = routes.shape
    capacity = rows * top // members + rows * top // (4 * members)
    per_peer = -(-(slot_count // members) // 16) * 16
    gate_proj, up_proj, down_proj = w_gate[0], w_up[0], w_down[0]

    def exchange(tensor):
        return lax.all_to_all(tensor, "dp", split_axis=0, concat_axis=0, tiled=True)

    ids = jnp.arange(members, dtype=jnp.int32)
    chosen = routes.T[None, :, :] == ids[:, None, None]
    named = jnp.any(chosen, axis=1)
    before = jnp.arange(rows)[:, None] < jnp.arange(rows)[None, :]
    place = jnp.dot(named.astype(BF), before.astype(BF), preferred_element_type=F32)
    place = jnp.where(named, place.astype(jnp.int32), -1)
    slots = jnp.arange(capacity, dtype=jnp.int32)
    hot = place[:, None, :] == slots[None, :, None]
    pack = hot.astype(BF).reshape(members * capacity, rows)
    shipped_grad = exchange(select(pack, cotangent).reshape(members, capacity, part))

    all_counts = lax.all_gather(row_counts, "dp", axis=0, tiled=True)
    starts = jnp.sum(jnp.where(ids[None, :] < ids[:, None], all_counts[None, :], 0), axis=1)
    my_start = starts[myself]
    my_count = all_counts[myself]
    column = jnp.arange(per_peer, dtype=jnp.int32)
    source_slot = (ids[:, None] - my_start) % members + column[None, :] * members
    source_slot = jnp.where(source_slot < my_count, source_slot, -1).reshape(-1)
    spread = (source_slot[:, None] == jnp.arange(slot_count, dtype=jnp.int32)[None, :]).astype(BF)
    incoming = exchange(select(spread, arrived_rows).reshape(members, per_peer, part))
    offset = (jnp.arange(rows, dtype=jnp.int32) * members + myself)[:, None] - starts[None, :]
    held = (offset >= 0) & (offset < all_counts[None, :])
    taken = jnp.where(held, offset // members, -1)
    take = (taken[:, :, None] == column[None, None, :]).astype(BF).reshape(rows, -1)
    balanced = select(take, incoming.reshape(-1, part))
    shipped = exchange(select(pack, balanced).reshape(members, capacity, part))

    tp = lax.axis_size("tp")

    def reduced(partial):
        return ring_scatter(rounded(partial).reshape(tp, -1, partial.shape[1]))

    both_proj = jnp.concatenate([gate_proj, up_proj], axis=1)
    shipped_grad, both_proj = lax.optimization_barrier((shipped_grad, both_proj))
    hidden_grad = reduced(dot_nt(shipped_grad.reshape(-1, part), down_proj))
    flat = shipped.reshape(-1, part)
    gate_pre = reduced(jnp.dot(flat, gate_proj, preferred_element_type=F32))
    up_pre = reduced(jnp.dot(flat, up_proj, preferred_element_type=F32))
    sigmoid_gate = jax.nn.sigmoid(gate_pre)
    hidden = (gate_pre * sigmoid_gate * up_pre).astype(BF)
    gate_grad = (
        hidden_grad * up_pre * sigmoid_gate * (1.0 + gate_pre * (1.0 - sigmoid_gate))
    ).astype(BF)
    up_grad = (hidden_grad * gate_pre * sigmoid_gate).astype(BF)
    hidden = ring_gather(hidden).reshape(members * capacity, -1)
    inner = jnp.concatenate([gate_grad, up_grad], axis=1).reshape(members // tp, capacity, -1)
    early = 24

    def gathered(group):
        return ring_gather(group.reshape(-1, group.shape[2])).reshape(-1, group.shape[2])

    scale_high = lax.optimization_barrier(gate_scale.astype(BF))
    scale_low = (gate_scale - scale_high.astype(F32)).astype(BF)

    def weights(scale):
        per_expert = jnp.sum(jnp.where(chosen, scale.astype(F32).T[None], 0.0), axis=1)
        return jnp.where(hot, per_expert[:, None, :], 0.0).astype(BF).reshape(-1, rows)

    mix = jnp.concatenate([weights(scale_high), weights(scale_low)], axis=1)
    mix = mix.reshape(members, capacity, -1)

    def combine(mix, returned):
        both = lax.dot_general(
            mix.reshape(-1, mix.shape[2]),
            returned.reshape(-1, part),
            (((0,), (0,)), ((), ())),
            preferred_element_type=F32,
        )
        return both[:rows] + both[rows:]

    expert_out = jnp.dot(hidden, down_proj, preferred_element_type=F32).astype(BF)
    returned_out = exchange(expert_out.reshape(members, capacity, part))

    def returned_grad(group):
        input_grad = dot_nt(gathered(group), both_proj).astype(BF)
        return exchange(input_grad.reshape(members, -1, part))

    first = returned_grad(inner[:, :early])
    second = returned_grad(inner[:, early:])
    balanced_grad = (combine(mix[:, :early], first) + combine(mix[:, early:], second)).astype(BF)
    leaving = select_t(take, balanced_grad)
    arriving = exchange(leaving.reshape(members, per_peer, part))
    grad_rows = select_t(spread, arriving.reshape(-1, part))
    layer_out = combine(mix, returned_out).astype(BF)
    return (layer_out, grad_rows)


def solution(mesh):
    placed = (
        P("dp", "tp"),
        P("dp"),
        P("dp", None),
        P("dp", None),
        P("dp", "tp", None),
        P("dp", "tp", None),
        P("dp", None, "tp"),
        P("dp", "tp"),
    )
    return jax.shard_map(
        on_device,
        mesh=mesh,
        in_specs=placed,
        out_specs=(P("dp", "tp"), P("dp", "tp")),
        check_vma=False,
    )
```

```python
import jax
import jax.numpy as jnp
from jax import lax
from jax.sharding import PartitionSpec as P

BF = jnp.bfloat16
F32 = jnp.float32


def rounded(tensor):
    return lax.optimization_barrier(tensor.astype(BF))


def select(left, right):
    return jnp.dot(left, right, preferred_element_type=F32).astype(BF)


def select_t(left, right):
    return lax.dot_general(
        left, right, (((0,), (0,)), ((), ())), preferred_element_type=F32
    ).astype(BF)


def dot_nt(left, right):
    return lax.dot_general(left, right, (((1,), (1,)), ((), ())), preferred_element_type=F32)


def f32(tensor):
    return tensor.astype(F32)


def ring_steps():
    size = lax.axis_size("tp")
    up = [(i, (i + 1) % size) for i in range(size)]
    down = [(i, (i - 1) % size) for i in range(size)]
    return (
        lambda t: lax.ppermute(t, "tp", up),
        lambda t: lax.ppermute(t, "tp", down),
        size,
    )


def ring_scatter(tensor, marks, far_up):
    send_up, send_down, size = ring_steps()
    me = lax.axis_index("tp")
    half = size // 2

    def own(k):
        return lax.dynamic_index_in_dim(tensor, k % size, 0, keepdims=False)

    a = b = None
    for s in range(half, 0, -1):
        if s < half or far_up:
            a = own(me + s) if a is None else (f32(a) + f32(own(me + s))).astype(BF)
        if s < half or not far_up:
            b = own(me - s) if b is None else (f32(b) + f32(own(me - s))).astype(BF)
        marks.append([v for v in (a, b) if v is not None])
        a = None if a is None else send_up(a)
        b = None if b is None else send_down(b)
    return f32(own(me)) + f32(a) + f32(b)


def ring_gather(shard, marks, far_up):
    send_up, send_down, size = ring_steps()
    me = lax.axis_index("tp")
    half = size // 2
    whole = jnp.zeros((size,) + shard.shape, shard.dtype)

    def put(whole, piece, k):
        return lax.dynamic_update_slice(whole, piece[None], (k % size, 0, 0))

    whole = put(whole, shard, me)
    a = b = shard
    for s in range(1, half):
        a, b = send_up(a), send_down(b)
        marks.append([a, b])
        whole = put(put(whole, a, me - s), b, me + s)
    return put(whole, send_up(a) if far_up else send_down(b), me + half)


def after(tensor, *others):
    return lax.optimization_barrier((tensor, others))[0]


def on_device(arrived_rows, row_counts, routes, gate_scale, w_gate, w_up, w_down, cotangent):
    members = lax.axis_size("dp")
    myself = lax.axis_index("dp")
    slot_count, part = arrived_rows.shape
    rows, top = routes.shape
    capacity = rows * top // members + rows * top // (4 * members)
    per_peer = -(-(slot_count // members) // 16) * 16
    gate_proj, up_proj, down_proj = w_gate[0], w_up[0], w_down[0]

    def exchange(tensor):
        return lax.all_to_all(tensor, "dp", split_axis=0, concat_axis=0, tiled=True)

    ids = jnp.arange(members, dtype=jnp.int32)
    chosen = routes.T[None, :, :] == ids[:, None, None]
    named = jnp.any(chosen, axis=1)
    before = jnp.arange(rows)[:, None] < jnp.arange(rows)[None, :]
    place = jnp.dot(named.astype(BF), before.astype(BF), preferred_element_type=F32)
    place = jnp.where(named, place.astype(jnp.int32), -1)
    slots = jnp.arange(capacity, dtype=jnp.int32)
    hot = place[:, None, :] == slots[None, :, None]
    early = 24

    def pack(rows_in, first, last):
        chosen_slots = hot[:, first:last].astype(BF).reshape(-1, rows)
        return select(chosen_slots, rows_in).reshape(members, last - first, part)

    packed_grad = pack(cotangent, 0, capacity)
    shipped_grad = exchange(packed_grad)
    row_counts = after(row_counts, packed_grad)

    all_counts = lax.all_gather(row_counts, "dp", axis=0, tiled=True)
    starts = jnp.sum(jnp.where(ids[None, :] < ids[:, None], all_counts[None, :], 0), axis=1)
    my_start = starts[myself]
    my_count = all_counts[myself]
    column = jnp.arange(per_peer, dtype=jnp.int32)
    source_slot = (ids[:, None] - my_start) % members + column[None, :] * members
    source_slot = jnp.where(source_slot < my_count, source_slot, -1).reshape(-1)
    spread = (source_slot[:, None] == jnp.arange(slot_count, dtype=jnp.int32)[None, :]).astype(BF)
    outgoing = select(spread, arrived_rows).reshape(members, per_peer, part)
    incoming = exchange(outgoing)
    shipped_grad = after(shipped_grad, outgoing)
    grad_part = rounded(dot_nt(shipped_grad.reshape(-1, part), down_proj))
    incoming = after(incoming, grad_part)
    hidden_grad = lax.psum_scatter(grad_part, "tp", scatter_dimension=0, tiled=True)
    tp = lax.axis_size("tp")
    width = hidden_grad.shape[1]
    hidden_grad = hidden_grad.reshape(members // tp, capacity, width)
    offset = (jnp.arange(rows, dtype=jnp.int32) * members + myself)[:, None] - starts[None, :]
    held = (offset >= 0) & (offset < all_counts[None, :])
    taken = jnp.where(held, offset // members, -1)
    take = (taken[:, :, None] == column[None, None, :]).astype(BF).reshape(rows, -1)
    balanced = select(take, incoming.reshape(-1, part))
    both_proj = jnp.concatenate([gate_proj, up_proj], axis=1)
    shipped = exchange(pack(balanced, 0, capacity))
    shipped, both_proj, hidden_grad = lax.optimization_barrier((shipped, both_proj, hidden_grad))
    first_shipped, second_shipped = shipped[:, :early], shipped[:, early:]

    def projected(shipped):
        flat = shipped.reshape(-1, part)
        both = rounded(jnp.dot(flat, both_proj, preferred_element_type=F32))
        return both.reshape(tp, -1, 2 * width)

    def activated(pre, hidden_grad, marks, far_up):
        hidden_grad = f32(hidden_grad).reshape(-1, width)
        gate_pre, up_pre = pre[:, :width], pre[:, width:]
        sigmoid_gate = jax.nn.sigmoid(gate_pre)
        hidden = (gate_pre * sigmoid_gate * up_pre).astype(BF)
        gate_grad = (
            hidden_grad * up_pre * sigmoid_gate * (1.0 + gate_pre * (1.0 - sigmoid_gate))
        ).astype(BF)
        up_grad = (hidden_grad * gate_pre * sigmoid_gate).astype(BF)
        inner = jnp.concatenate([gate_grad, up_grad, hidden], axis=1)
        return ring_gather(inner, marks, far_up).reshape(-1, 3 * width)

    marks_a, marks_b, marks_c, marks_d = [], [], [], []
    first_part = projected(first_shipped)
    second_part = projected(after(second_shipped, first_part))
    first_pre = ring_scatter(first_part, marks_a, True)
    second_pre = ring_scatter(second_part, marks_b, False)
    first_inner = activated(first_pre, hidden_grad[:, :early], marks_c, True)
    second_pre = after(second_pre, *marks_c[0])
    second_inner = activated(second_pre, hidden_grad[:, early:], marks_d, False)
    first_inner = after(first_inner, *marks_d[2])

    def returned(inner):
        input_grad = dot_nt(inner[:, : 2 * width], both_proj).astype(BF)
        expert_out = jnp.dot(inner[:, 2 * width :], down_proj, preferred_element_type=F32)
        split = (members, -1, part)
        both = jnp.concatenate(
            [input_grad.reshape(split), expert_out.astype(BF).reshape(split)], axis=1
        )
        return both

    def parted(both):
        return both[:, : both.shape[1] // 2], both[:, both.shape[1] // 2 :]

    first_both = returned(first_inner)
    second_both = returned(after(second_inner, first_both))
    first_both = exchange(first_both)
    first_grad, first_out = parted(first_both)
    second_grad, second_out = parted(exchange(after(second_both, first_both)))

    scale_high = lax.optimization_barrier(gate_scale.astype(BF))
    scale_low = (gate_scale - scale_high.astype(F32)).astype(BF)

    def weights(scale):
        per_expert = jnp.sum(jnp.where(chosen, scale.astype(F32).T[None], 0.0), axis=1)
        return jnp.where(hot, per_expert[:, None, :], 0.0).astype(BF).reshape(-1, rows)

    mix = jnp.concatenate([weights(scale_high), weights(scale_low)], axis=1)
    mix = mix.reshape(members, capacity, -1)

    def combine(mix, returned):
        both = lax.dot_general(
            mix.reshape(-1, mix.shape[2]),
            returned.reshape(-1, part),
            (((0,), (0,)), ((), ())),
            preferred_element_type=F32,
        )
        return both[:rows] + both[rows:]

    def mixed(first, second):
        return (combine(mix[:, :early], first) + combine(mix[:, early:], second)).astype(BF)

    balanced_grad = mixed(first_grad, second_grad)
    leaving = select_t(take, balanced_grad)
    arriving = exchange(leaving.reshape(members, per_peer, part))
    grad_rows = select_t(spread, arriving.reshape(-1, part))
    layer_out = mixed(first_out, second_out)
    return (layer_out, grad_rows)


def solution(mesh):
    placed = (
        P("dp", "tp"),
        P("dp"),
        P("dp", None),
        P("dp", None),
        P("dp", "tp", None),
        P("dp", "tp", None),
        P("dp", None, "tp"),
        P("dp", "tp"),
    )
    return jax.shard_map(
        on_device,
        mesh=mesh,
        in_specs=placed,
        out_specs=(P("dp", "tp"), P("dp", "tp")),
        check_vma=False,
    )
```

```python
import jax
import jax.numpy as jnp
from jax import lax
from jax.sharding import PartitionSpec as P

BF = jnp.bfloat16
F32 = jnp.float32


def rounded(tensor):
    return lax.optimization_barrier(tensor.astype(BF))


def select(left, right):
    return jnp.dot(left, right, preferred_element_type=F32).astype(BF)


def select_t(left, right):
    return lax.dot_general(
        left, right, (((0,), (0,)), ((), ())), preferred_element_type=F32
    ).astype(BF)


def dot_nt(left, right):
    return lax.dot_general(left, right, (((1,), (1,)), ((), ())), preferred_element_type=F32)


def f32(tensor):
    return tensor.astype(F32)


def after(tensor, *others):
    return lax.optimization_barrier((tensor, others))[0]


def ring_steps():
    size = lax.axis_size("tp")
    up = [(i, (i + 1) % size) for i in range(size)]
    down = [(i, (i - 1) % size) for i in range(size)]
    return (
        lambda t: lax.ppermute(t, "tp", up),
        lambda t: lax.ppermute(t, "tp", down),
        size,
    )


def ring_scatter(tensor, marks, far_up, gate=None):
    send_up, send_down, size = ring_steps()
    me = lax.axis_index("tp")
    half = size // 2

    def own(k):
        return lax.dynamic_index_in_dim(tensor, k % size, 0, keepdims=False)

    a = b = None
    for s in range(half, 0, -1):
        if s < half or far_up:
            a = own(me + s) if a is None else (f32(a) + f32(own(me + s))).astype(BF)
        if s < half or not far_up:
            b = own(me - s) if b is None else (f32(b) + f32(own(me - s))).astype(BF)
        if gate is not None and s == gate[0]:
            a, b = after((a, b), *gate[1])
        marks.append([v for v in (a, b) if v is not None])
        a = None if a is None else send_up(a)
        b = None if b is None else send_down(b)
    return f32(own(me)) + f32(a) + f32(b)


def ring_gather(shard, marks, far_up):
    send_up, send_down, size = ring_steps()
    me = lax.axis_index("tp")
    half = size // 2
    whole = jnp.zeros((size,) + shard.shape, shard.dtype)

    def put(whole, piece, k):
        return lax.dynamic_update_slice(whole, piece[None], (k % size, 0, 0))

    whole = put(whole, shard, me)
    a = b = shard
    for s in range(1, half):
        a, b = send_up(a), send_down(b)
        marks.append([a, b])
        whole = put(put(whole, a, me - s), b, me + s)
    return put(whole, send_up(a) if far_up else send_down(b), me + half)


def on_device(arrived_rows, row_counts, routes, gate_scale, w_gate, w_up, w_down, cotangent):
    members = lax.axis_size("dp")
    myself = lax.axis_index("dp")
    slot_count, part = arrived_rows.shape
    rows, top = routes.shape
    capacity = rows * top // members + rows * top // (4 * members)
    per_peer = -(-(slot_count // members) // 16) * 16
    gate_proj, up_proj, down_proj = w_gate[0], w_up[0], w_down[0]

    def exchange(tensor):
        return lax.all_to_all(tensor, "dp", split_axis=0, concat_axis=0, tiled=True)

    ids = jnp.arange(members, dtype=jnp.int32)
    chosen = routes.T[None, :, :] == ids[:, None, None]
    named = jnp.any(chosen, axis=1)
    before = jnp.arange(rows)[:, None] < jnp.arange(rows)[None, :]
    place = jnp.dot(named.astype(BF), before.astype(BF), preferred_element_type=F32)
    place = jnp.where(named, place.astype(jnp.int32), -1)
    slots = jnp.arange(capacity, dtype=jnp.int32)
    hot = place[:, None, :] == slots[None, :, None]
    early = 24

    def pack(rows_in, first, last):
        chosen_slots = hot[:, first:last].astype(BF).reshape(-1, rows)
        return select(chosen_slots, rows_in).reshape(members, last - first, part)

    packed_grad = pack(cotangent, 0, capacity)

    all_counts = lax.all_gather(row_counts, "dp", axis=0, tiled=True)
    starts = jnp.sum(jnp.where(ids[None, :] < ids[:, None], all_counts[None, :], 0), axis=1)
    my_start = starts[myself]
    my_count = all_counts[myself]
    column = jnp.arange(per_peer, dtype=jnp.int32)
    source_slot = (ids[:, None] - my_start) % members + column[None, :] * members
    source_slot = jnp.where(source_slot < my_count, source_slot, -1).reshape(-1)
    spread = (source_slot[:, None] == jnp.arange(slot_count, dtype=jnp.int32)[None, :]).astype(BF)
    outgoing = select(spread, arrived_rows).reshape(members, per_peer, part)
    incoming = exchange(outgoing)
    offset = (jnp.arange(rows, dtype=jnp.int32) * members + myself)[:, None] - starts[None, :]
    held = (offset >= 0) & (offset < all_counts[None, :])
    taken = jnp.where(held, offset // members, -1)
    take = (taken[:, :, None] == column[None, None, :]).astype(BF).reshape(rows, -1)
    balanced = select(take, incoming.reshape(-1, part))
    tp = lax.axis_size("tp")
    width = gate_proj.shape[1]
    shipped = exchange(pack(balanced, 0, capacity))
    shipped_grad = exchange(after(packed_grad, shipped))
    both_proj = jnp.concatenate([gate_proj, up_proj], axis=1)
    shipped, both_proj = lax.optimization_barrier((shipped, both_proj))

    def by_shard(partial):
        return rounded(partial).reshape(tp, -1, width)

    flat = shipped.reshape(-1, part)
    gate_part = by_shard(jnp.dot(flat, gate_proj, preferred_element_type=F32))
    flat = after(flat, gate_part)
    up_part = by_shard(jnp.dot(flat, up_proj, preferred_element_type=F32))
    grad_part = by_shard(dot_nt(shipped_grad.reshape(-1, part), down_proj))
    marks_g, marks_u, marks_h, marks_o, marks_a, marks_b = [], [], [], [], [], []
    gate_pre = ring_scatter(gate_part, marks_g, True, (2, (grad_part,)))
    up_pre = ring_scatter(up_part, marks_u, False)
    hidden_grad = ring_scatter(grad_part, marks_h, True)

    sigmoid_gate = jax.nn.sigmoid(gate_pre)
    hidden = (gate_pre * sigmoid_gate * up_pre).astype(BF)
    hidden = after(hidden, *marks_h[1])
    gate_pre, up_pre, sigmoid_gate = after((gate_pre, up_pre, sigmoid_gate), hidden)
    hidden = ring_gather(hidden, marks_o, False).reshape(-1, width)
    gate_grad = (
        hidden_grad * up_pre * sigmoid_gate * (1.0 + gate_pre * (1.0 - sigmoid_gate))
    ).astype(BF)
    up_grad = (hidden_grad * gate_pre * sigmoid_gate).astype(BF)
    inner = jnp.concatenate([gate_grad, up_grad], axis=1).reshape(-1, capacity, 2 * width)
    first = after(inner[:, :early], *marks_o[1]).reshape(-1, 2 * width)
    first = ring_gather(first, marks_a, True).reshape(-1, 2 * width)
    second = after(inner[:, early:], *marks_a[1]).reshape(-1, 2 * width)
    second = ring_gather(second, marks_b, False).reshape(-1, 2 * width)

    split = (members, -1, part)
    expert_out = jnp.dot(hidden, down_proj, preferred_element_type=F32).astype(BF)
    returned_out = exchange(expert_out.reshape(split))
    first = after(first, expert_out, *marks_b[1])
    first_grad = dot_nt(first, both_proj).astype(BF)
    second = after(second, first_grad)
    first_grad = exchange(after(first_grad, returned_out).reshape(split))
    second_grad = dot_nt(second, both_proj).astype(BF)
    second_grad = exchange(after(second_grad, first_grad).reshape(split))

    scale_high = lax.optimization_barrier(gate_scale.astype(BF))
    scale_low = (gate_scale - scale_high.astype(F32)).astype(BF)

    def weights(scale):
        per_expert = jnp.sum(jnp.where(chosen, scale.astype(F32).T[None], 0.0), axis=1)
        return jnp.where(hot, per_expert[:, None, :], 0.0).astype(BF).reshape(-1, rows)

    mix = jnp.concatenate([weights(scale_high), weights(scale_low)], axis=1)
    mix = mix.reshape(members, capacity, -1)

    def combine(mix, returned):
        both = lax.dot_general(
            mix.reshape(-1, mix.shape[2]),
            returned.reshape(-1, part),
            (((0,), (0,)), ((), ())),
            preferred_element_type=F32,
        )
        return both[:rows] + both[rows:]

    balanced_grad = combine(mix[:, :early], first_grad) + combine(mix[:, early:], second_grad)
    balanced_grad = balanced_grad.astype(BF)
    leaving = select_t(take, balanced_grad)
    arriving = exchange(leaving.reshape(members, per_peer, part))
    grad_rows = select_t(spread, arriving.reshape(-1, part))
    layer_out = combine(mix, returned_out).astype(BF)
    return (layer_out, grad_rows)


def solution(mesh):
    placed = (
        P("dp", "tp"),
        P("dp"),
        P("dp", None),
        P("dp", None),
        P("dp", "tp", None),
        P("dp", "tp", None),
        P("dp", None, "tp"),
        P("dp", "tp"),
    )
    return jax.shard_map(
        on_device,
        mesh=mesh,
        in_specs=placed,
        out_specs=(P("dp", "tp"), P("dp", "tp")),
        check_vma=False,
    )
```

```python
import jax
import jax.numpy as jnp
from jax import lax
from jax.sharding import PartitionSpec as P

BF = jnp.bfloat16
F32 = jnp.float32


def rounded(tensor):
    return lax.optimization_barrier(tensor.astype(BF))


def select(left, right):
    return jnp.dot(left, right, preferred_element_type=F32).astype(BF)


def select_t(left, right):
    return lax.dot_general(
        left, right, (((0,), (0,)), ((), ())), preferred_element_type=F32
    ).astype(BF)


def dot_nt(left, right):
    return lax.dot_general(left, right, (((1,), (1,)), ((), ())), preferred_element_type=F32)


def f32(tensor):
    return tensor.astype(F32)


def after(tensor, *others):
    return lax.optimization_barrier((tensor, others))[0]


def ring_steps():
    size = lax.axis_size("tp")
    up = [(i, (i + 1) % size) for i in range(size)]
    down = [(i, (i - 1) % size) for i in range(size)]
    return (
        lambda t: lax.ppermute(t, "tp", up),
        lambda t: lax.ppermute(t, "tp", down),
        size,
    )


def ring_scatter(tensor, marks, far_up, gate=None):
    send_up, send_down, size = ring_steps()
    me = lax.axis_index("tp")
    half = size // 2

    def own(k):
        return lax.dynamic_index_in_dim(tensor, k % size, 0, keepdims=False)

    a = b = None
    for s in range(half, 0, -1):
        if s < half or far_up:
            a = own(me + s) if a is None else (f32(a) + f32(own(me + s))).astype(BF)
        if s < half or not far_up:
            b = own(me - s) if b is None else (f32(b) + f32(own(me - s))).astype(BF)
        if gate is not None and s == gate[0]:
            a, b = after((a, b), gate[1]())
        marks.append([v for v in (a, b) if v is not None])
        a = None if a is None else send_up(a)
        b = None if b is None else send_down(b)
    return f32(own(me)) + f32(a) + f32(b)


def ring_gather(shards, marks, ways):
    send_up, send_down, size = ring_steps()
    me = lax.axis_index("tp")
    half = size // 2
    rows, width = shards[0].shape
    whole = jnp.zeros((size, rows, width * len(shards)), BF)

    def put(whole, piece, k, n):
        return lax.dynamic_update_slice(whole, piece[None], (k % size, 0, n * width))

    pairs = [(shard, shard) for shard in shards]
    for n, shard in enumerate(shards):
        whole = put(whole, shard, me, n)
    for s in range(1, half):
        pairs = [(send_up(a), send_down(b)) for a, b in pairs]
        marks.append([v for pair in pairs for v in pair])
        for n, (a, b) in enumerate(pairs):
            whole = put(put(whole, a, me - s, n), b, me + s, n)
    for n, (a, b) in enumerate(pairs):
        whole = put(whole, send_up(a) if ways[n] else send_down(b), me + half, n)
    return whole.reshape(size * rows, -1)


def on_device(arrived_rows, row_counts, routes, gate_scale, w_gate, w_up, w_down, cotangent):
    members = lax.axis_size("dp")
    myself = lax.axis_index("dp")
    slot_count, part = arrived_rows.shape
    rows, top = routes.shape
    capacity = rows * top // members + rows * top // (4 * members)
    per_peer = -(-(slot_count // members) // 16) * 16
    gate_proj, up_proj, down_proj = w_gate[0], w_up[0], w_down[0]

    def exchange(tensor):
        return lax.all_to_all(tensor, "dp", split_axis=0, concat_axis=0, tiled=True)

    ids = jnp.arange(members, dtype=jnp.int32)
    chosen = routes.T[None, :, :] == ids[:, None, None]
    named = jnp.any(chosen, axis=1)
    before = jnp.arange(rows)[:, None] < jnp.arange(rows)[None, :]
    place = jnp.dot(named.astype(BF), before.astype(BF), preferred_element_type=F32)
    place = jnp.where(named, place.astype(jnp.int32), -1)
    slots = jnp.arange(capacity, dtype=jnp.int32)
    hot = place[:, None, :] == slots[None, :, None]
    def pack(rows_in, first, last):
        chosen_slots = hot[:, first:last].astype(BF).reshape(-1, rows)
        return select(chosen_slots, rows_in).reshape(members, last - first, part)

    packed_grad = pack(cotangent, 0, capacity)

    all_counts = exchange(jnp.broadcast_to(row_counts, (members, 1, 128)))[:, 0, 0]
    starts = jnp.sum(jnp.where(ids[None, :] < ids[:, None], all_counts[None, :], 0), axis=1)
    my_start = starts[myself]
    my_count = all_counts[myself]
    column = jnp.arange(per_peer, dtype=jnp.int32)
    source_slot = (ids[:, None] - my_start) % members + column[None, :] * members
    source_slot = jnp.where(source_slot < my_count, source_slot, -1).reshape(-1)
    spread = (source_slot[:, None] == jnp.arange(slot_count, dtype=jnp.int32)[None, :]).astype(BF)
    outgoing = select(spread, arrived_rows).reshape(members, per_peer, part)
    incoming = exchange(outgoing)
    both_proj = jnp.concatenate([gate_proj, up_proj], axis=1)
    incoming, both_proj, packed_grad = lax.optimization_barrier(
        (incoming, both_proj, packed_grad)
    )
    offset = (jnp.arange(rows, dtype=jnp.int32) * members + myself)[:, None] - starts[None, :]
    held = (offset >= 0) & (offset < all_counts[None, :])
    taken = jnp.where(held, offset // members, -1)
    take = (taken[:, :, None] == column[None, None, :]).astype(BF).reshape(rows, -1)
    balanced = select(take, incoming.reshape(-1, part))
    tp = lax.axis_size("tp")
    width = gate_proj.shape[1]
    shipped = exchange(pack(balanced, 0, capacity))
    shipped_grad = exchange(after(packed_grad, shipped))

    def by_shard(partial):
        return rounded(partial).reshape(tp, -1, width)

    flat = shipped.reshape(-1, part)
    gate_part = by_shard(jnp.dot(flat, gate_proj, preferred_element_type=F32))
    flat = after(flat, gate_part)
    up_part = by_shard(jnp.dot(flat, up_proj, preferred_element_type=F32))
    marks_u, marks_h, marks_o, marks_i = [], [], [], []
    gate_pre = f32(
        lax.psum_scatter(gate_part.reshape(-1, width), "tp", scatter_dimension=0, tiled=True)
    )
    grad_parts = []

    def grad_part():
        arrived = after(shipped_grad, *marks_u[2]).reshape(-1, part)
        grad_parts.append(by_shard(dot_nt(arrived, down_proj)))
        return grad_parts[0]

    up_pre = ring_scatter(up_part, marks_u, True, (1, grad_part))
    hidden_grad = ring_scatter(grad_parts[0], marks_h, False)

    sigmoid_gate = jax.nn.sigmoid(gate_pre)
    hidden = (gate_pre * sigmoid_gate * up_pre).astype(BF)
    hidden = after(hidden, *marks_h[1])
    gate_pre, up_pre, sigmoid_gate = after((gate_pre, up_pre, sigmoid_gate), hidden)
    hidden = ring_gather([hidden], marks_o, [True])
    gate_grad = (
        hidden_grad * up_pre * sigmoid_gate * (1.0 + gate_pre * (1.0 - sigmoid_gate))
    ).astype(BF)
    up_grad = (hidden_grad * gate_pre * sigmoid_gate).astype(BF)
    gate_grad, up_grad = after((gate_grad, up_grad), *marks_o[1])
    inner = ring_gather([gate_grad, up_grad], marks_i, [False, True])

    split = (members, -1, part)
    expert_out = jnp.dot(hidden, down_proj, preferred_element_type=F32).astype(BF)
    returned_out = exchange(expert_out.reshape(split))
    input_grad = dot_nt(after(inner, expert_out), both_proj).astype(BF)
    returned_grad = exchange(after(input_grad, returned_out).reshape(split))

    scale_high = lax.optimization_barrier(gate_scale.astype(BF))
    scale_low = (gate_scale - scale_high.astype(F32)).astype(BF)

    def weights(scale):
        per_expert = jnp.sum(jnp.where(chosen, scale.astype(F32).T[None], 0.0), axis=1)
        return jnp.where(hot, per_expert[:, None, :], 0.0).astype(BF).reshape(-1, rows)

    mix = jnp.concatenate([weights(scale_high), weights(scale_low)], axis=1)
    mix = mix.reshape(members, capacity, -1)

    def combine(mix, returned):
        both = lax.dot_general(
            mix.reshape(-1, mix.shape[2]),
            returned.reshape(-1, part),
            (((0,), (0,)), ((), ())),
            preferred_element_type=F32,
        )
        return both[:rows] + both[rows:]

    balanced_grad = combine(mix, returned_grad).astype(BF)
    leaving = select_t(take, balanced_grad)
    arriving = exchange(leaving.reshape(members, per_peer, part))
    grad_rows = select_t(spread, arriving.reshape(-1, part))
    layer_out = combine(mix, returned_out).astype(BF)
    return (layer_out, grad_rows)


def solution(mesh):
    placed = (
        P("dp", "tp"),
        P("dp"),
        P("dp", None),
        P("dp", None),
        P("dp", "tp", None),
        P("dp", "tp", None),
        P("dp", None, "tp"),
        P("dp", "tp"),
    )
    return jax.shard_map(
        on_device,
        mesh=mesh,
        in_specs=placed,
        out_specs=(P("dp", "tp"), P("dp", "tp")),
        check_vma=False,
    )
```

```python
import jax
import jax.numpy as jnp
from jax import lax
from jax.sharding import PartitionSpec as P

BF = jnp.bfloat16
F32 = jnp.float32


def rounded(tensor):
    return lax.optimization_barrier(tensor.astype(BF))


def select(left, right):
    return jnp.dot(left, right, preferred_element_type=F32).astype(BF)


def select_t(left, right):
    return lax.dot_general(
        left, right, (((0,), (0,)), ((), ())), preferred_element_type=F32
    ).astype(BF)


def dot_nt(left, right):
    return lax.dot_general(left, right, (((1,), (1,)), ((), ())), preferred_element_type=F32)


def f32(tensor):
    return tensor.astype(F32)


def after(tensor, *others):
    return lax.optimization_barrier((tensor, others))[0]


def ring_steps():
    size = lax.axis_size("tp")
    up = [(i, (i + 1) % size) for i in range(size)]
    down = [(i, (i - 1) % size) for i in range(size)]
    return (
        lambda t: lax.ppermute(t, "tp", up),
        lambda t: lax.ppermute(t, "tp", down),
        size,
    )


def ring_scatter(tensor, marks, far_up, gate=None):
    send_up, send_down, size = ring_steps()
    me = lax.axis_index("tp")
    half = size // 2

    def own(k):
        return lax.dynamic_index_in_dim(tensor, k % size, 0, keepdims=False)

    a = b = None
    for s in range(half, 0, -1):
        if s < half or far_up:
            a = own(me + s) if a is None else (f32(a) + f32(own(me + s))).astype(BF)
        if s < half or not far_up:
            b = own(me - s) if b is None else (f32(b) + f32(own(me - s))).astype(BF)
        if gate is not None and s == 1:
            a, b = after((a, b), gate())
        marks.append([v for v in (a, b) if v is not None])
        a = None if a is None else send_up(a)
        b = None if b is None else send_down(b)
    return f32(own(me)) + f32(a) + f32(b)


def ring_gather(shard, marks, far_up):
    send_up, send_down, size = ring_steps()
    me = lax.axis_index("tp")
    half = size // 2
    whole = jnp.zeros((size,) + shard.shape, shard.dtype)

    def put(whole, piece, k):
        return lax.dynamic_update_slice(whole, piece[None], (k % size, 0, 0))

    whole = put(whole, shard, me)
    a = b = shard
    for s in range(1, half):
        a, b = send_up(a), send_down(b)
        marks.append([a, b])
        whole = put(put(whole, a, me - s), b, me + s)
    return put(whole, send_up(a) if far_up else send_down(b), me + half)


def on_device(arrived_rows, row_counts, routes, gate_scale, w_gate, w_up, w_down, cotangent):
    members = lax.axis_size("dp")
    myself = lax.axis_index("dp")
    slot_count, part = arrived_rows.shape
    rows, top = routes.shape
    capacity = rows * top // members + rows * top // (4 * members)
    per_peer = -(-(slot_count // members) // 16) * 16
    gate_proj, up_proj, down_proj = w_gate[0], w_up[0], w_down[0]

    def exchange(tensor):
        return lax.all_to_all(tensor, "dp", split_axis=0, concat_axis=0, tiled=True)

    ids = jnp.arange(members, dtype=jnp.int32)
    chosen = routes.T[None, :, :] == ids[:, None, None]
    named = jnp.any(chosen, axis=1)
    before = jnp.arange(rows)[:, None] < jnp.arange(rows)[None, :]
    place = jnp.dot(named.astype(BF), before.astype(BF), preferred_element_type=F32)
    place = jnp.where(named, place.astype(jnp.int32), -1)
    slots = jnp.arange(capacity, dtype=jnp.int32)
    hot = place[:, None, :] == slots[None, :, None]
    early = 24

    def pack(rows_in, first, last):
        chosen_slots = hot[:, first:last].astype(BF).reshape(-1, rows)
        return select(chosen_slots, rows_in).reshape(members, last - first, part)

    packed_grad = pack(cotangent, 0, capacity)

    all_counts = exchange(jnp.broadcast_to(row_counts, (members, 1, 128)))[:, 0, 0]
    starts = jnp.sum(jnp.where(ids[None, :] < ids[:, None], all_counts[None, :], 0), axis=1)
    my_start = starts[myself]
    my_count = all_counts[myself]
    column = jnp.arange(per_peer, dtype=jnp.int32)
    source_slot = (ids[:, None] - my_start) % members + column[None, :] * members
    source_slot = jnp.where(source_slot < my_count, source_slot, -1).reshape(-1)
    spread = (source_slot[:, None] == jnp.arange(slot_count, dtype=jnp.int32)[None, :]).astype(BF)
    outgoing = select(spread, arrived_rows).reshape(members, per_peer, part)
    incoming = exchange(outgoing)
    both_proj = jnp.concatenate([gate_proj, up_proj], axis=1)
    incoming, both_proj, packed_grad = lax.optimization_barrier(
        (incoming, both_proj, packed_grad)
    )
    offset = (jnp.arange(rows, dtype=jnp.int32) * members + myself)[:, None] - starts[None, :]
    held = (offset >= 0) & (offset < all_counts[None, :])
    taken = jnp.where(held, offset // members, -1)
    take = (taken[:, :, None] == column[None, None, :]).astype(BF).reshape(rows, -1)
    balanced = select(take, incoming.reshape(-1, part))
    tp = lax.axis_size("tp")
    width = gate_proj.shape[1]
    shipped = exchange(pack(balanced, 0, capacity))
    shipped_grad = exchange(after(packed_grad, shipped))

    def by_shard(partial):
        return rounded(partial).reshape(tp, -1, width)

    flat = shipped.reshape(-1, part)
    gate_part = by_shard(jnp.dot(flat, gate_proj, preferred_element_type=F32))
    flat = after(flat, gate_part)
    up_part = by_shard(jnp.dot(flat, up_proj, preferred_element_type=F32))
    marks_g, marks_u, marks_h, marks_o, marks_a, marks_b = [], [], [], [], [], []
    grad_parts = []

    def grad_part():
        arrived = after(shipped_grad, *marks_g[2]).reshape(-1, part)
        grad_parts.append(by_shard(dot_nt(arrived, down_proj)))
        return grad_parts[0]

    gate_pre = ring_scatter(gate_part, marks_g, True, grad_part)
    up_pre = ring_scatter(up_part, marks_u, False)
    hidden_grad = ring_scatter(grad_parts[0], marks_h, True)

    sigmoid_gate = jax.nn.sigmoid(gate_pre)
    hidden = (gate_pre * sigmoid_gate * up_pre).astype(BF)
    hidden = after(hidden, *marks_h[1])
    gate_pre, up_pre, sigmoid_gate = after((gate_pre, up_pre, sigmoid_gate), hidden)
    hidden = ring_gather(hidden, marks_o, False).reshape(-1, width)
    gate_grad = (
        hidden_grad * up_pre * sigmoid_gate * (1.0 + gate_pre * (1.0 - sigmoid_gate))
    ).astype(BF)
    up_grad = (hidden_grad * gate_pre * sigmoid_gate).astype(BF)
    inner = jnp.concatenate([gate_grad, up_grad], axis=1).reshape(-1, capacity, 2 * width)
    first = after(inner[:, :early], *marks_o[1]).reshape(-1, 2 * width)
    first = ring_gather(first, marks_a, True).reshape(-1, 2 * width)
    second = after(inner[:, early:], *marks_a[1]).reshape(-1, 2 * width)
    second = ring_gather(second, marks_b, False).reshape(-1, 2 * width)

    split = (members, -1, part)
    expert_out = jnp.dot(hidden, down_proj, preferred_element_type=F32).astype(BF)
    returned_out = exchange(expert_out.reshape(split))
    first = after(first, expert_out, *marks_b[1])
    first_grad = dot_nt(first, both_proj).astype(BF)
    second = after(second, first_grad)
    first_grad = exchange(after(first_grad, returned_out).reshape(split))
    second_grad = dot_nt(second, both_proj).astype(BF)
    second_grad = exchange(after(second_grad, first_grad).reshape(split))

    scale_high = lax.optimization_barrier(gate_scale.astype(BF))
    scale_low = (gate_scale - scale_high.astype(F32)).astype(BF)

    def weights(scale):
        per_expert = jnp.sum(jnp.where(chosen, scale.astype(F32).T[None], 0.0), axis=1)
        return jnp.where(hot, per_expert[:, None, :], 0.0).astype(BF).reshape(-1, rows)

    mix = jnp.concatenate([weights(scale_high), weights(scale_low)], axis=1)
    mix = mix.reshape(members, capacity, -1)

    def combine(mix, returned):
        both = lax.dot_general(
            mix.reshape(-1, mix.shape[2]),
            returned.reshape(-1, part),
            (((0,), (0,)), ((), ())),
            preferred_element_type=F32,
        )
        return both[:rows] + both[rows:]

    balanced_grad = combine(mix[:, :early], first_grad) + combine(mix[:, early:], second_grad)
    balanced_grad = balanced_grad.astype(BF)
    leaving = select_t(take, balanced_grad)
    arriving = exchange(leaving.reshape(members, per_peer, part))
    grad_rows = select_t(spread, arriving.reshape(-1, part))
    layer_out = combine(mix, returned_out).astype(BF)
    return (layer_out, grad_rows)


def solution(mesh):
    placed = (
        P("dp", "tp"),
        P("dp"),
        P("dp", None),
        P("dp", None),
        P("dp", "tp", None),
        P("dp", "tp", None),
        P("dp", None, "tp"),
        P("dp", "tp"),
    )
    return jax.shard_map(
        on_device,
        mesh=mesh,
        in_specs=placed,
        out_specs=(P("dp", "tp"), P("dp", "tp")),
        check_vma=False,
    )
```

```python
import jax
import jax.numpy as jnp
from jax import lax
from jax.sharding import PartitionSpec as P

BF = jnp.bfloat16
F32 = jnp.float32


def rounded(tensor):
    return lax.optimization_barrier(tensor.astype(BF))


def select(left, right):
    return jnp.dot(left, right, preferred_element_type=F32).astype(BF)


def select_t(left, right):
    return lax.dot_general(
        left, right, (((0,), (0,)), ((), ())), preferred_element_type=F32
    ).astype(BF)


def dot_nt(left, right):
    return lax.dot_general(left, right, (((1,), (1,)), ((), ())), preferred_element_type=F32)


def f32(tensor):
    return tensor.astype(F32)


def after(tensor, *others):
    return lax.optimization_barrier((tensor, others))[0]


def ring_steps():
    size = lax.axis_size("tp")
    up = [(i, (i + 1) % size) for i in range(size)]
    down = [(i, (i - 1) % size) for i in range(size)]
    return (
        lambda t: lax.ppermute(t, "tp", up),
        lambda t: lax.ppermute(t, "tp", down),
        size,
    )


def ring_scatter(tensor, marks, far_up, gate=None):
    send_up, send_down, size = ring_steps()
    me = lax.axis_index("tp")
    half = size // 2

    def own(k):
        return lax.dynamic_index_in_dim(tensor, k % size, 0, keepdims=False)

    a = b = None
    for s in range(half, 0, -1):
        if s < half or far_up:
            a = own(me + s) if a is None else (f32(a) + f32(own(me + s))).astype(BF)
        if s < half or not far_up:
            b = own(me - s) if b is None else (f32(b) + f32(own(me - s))).astype(BF)
        if gate is not None and s == 1:
            a, b = after((a, b), gate())
        marks.append([v for v in (a, b) if v is not None])
        a = None if a is None else send_up(a)
        b = None if b is None else send_down(b)
    return f32(own(me)) + f32(a) + f32(b)


def ring_gather(shard, marks, far_up):
    send_up, send_down, size = ring_steps()
    me = lax.axis_index("tp")
    half = size // 2
    whole = jnp.zeros((size,) + shard.shape, shard.dtype)

    def put(whole, piece, k):
        return lax.dynamic_update_slice(whole, piece[None], (k % size, 0, 0))

    whole = put(whole, shard, me)
    a = b = shard
    for s in range(1, half):
        a, b = send_up(a), send_down(b)
        marks.append([a, b])
        whole = put(put(whole, a, me - s), b, me + s)
    return put(whole, send_up(a) if far_up else send_down(b), me + half)


def on_device(arrived_rows, row_counts, routes, gate_scale, w_gate, w_up, w_down, cotangent):
    members = lax.axis_size("dp")
    myself = lax.axis_index("dp")
    slot_count, part = arrived_rows.shape
    rows, top = routes.shape
    capacity = rows * top // members + rows * top // (4 * members)
    per_peer = -(-(slot_count // members) // 16) * 16
    gate_proj, up_proj, down_proj = w_gate[0], w_up[0], w_down[0]

    def exchange(tensor):
        return lax.all_to_all(tensor, "dp", split_axis=0, concat_axis=0, tiled=True)

    ids = jnp.arange(members, dtype=jnp.int32)
    chosen = routes.T[None, :, :] == ids[:, None, None]
    named = jnp.any(chosen, axis=1)
    before = jnp.arange(rows)[:, None] < jnp.arange(rows)[None, :]
    place = jnp.dot(named.astype(BF), before.astype(BF), preferred_element_type=F32)
    place = jnp.where(named, place.astype(jnp.int32), -1)
    slots = jnp.arange(capacity, dtype=jnp.int32)
    hot = place[:, None, :] == slots[None, :, None]
    early = 24

    def pack(rows_in, first, last):
        chosen_slots = hot[:, first:last].astype(BF).reshape(-1, rows)
        return select(chosen_slots, rows_in).reshape(members, last - first, part)

    packed_grad = pack(cotangent, 0, capacity)

    all_counts = exchange(jnp.broadcast_to(row_counts, (members, 1, 128)))[:, 0, 0]
    starts = jnp.sum(jnp.where(ids[None, :] < ids[:, None], all_counts[None, :], 0), axis=1)
    my_start = starts[myself]
    my_count = all_counts[myself]
    column = jnp.arange(per_peer, dtype=jnp.int32)
    source_slot = (ids[:, None] - my_start) % members + column[None, :] * members
    source_slot = jnp.where(source_slot < my_count, source_slot, -1).reshape(-1)
    spread = (source_slot[:, None] == jnp.arange(slot_count, dtype=jnp.int32)[None, :]).astype(BF)
    outgoing = select(spread, arrived_rows).reshape(members, per_peer, part)
    incoming = exchange(outgoing)
    both_proj = jnp.concatenate([gate_proj, up_proj], axis=1)
    incoming, both_proj, packed_grad = lax.optimization_barrier(
        (incoming, both_proj, packed_grad)
    )
    offset = (jnp.arange(rows, dtype=jnp.int32) * members + myself)[:, None] - starts[None, :]
    held = (offset >= 0) & (offset < all_counts[None, :])
    taken = jnp.where(held, offset // members, -1)
    take = (taken[:, :, None] == column[None, None, :]).astype(BF).reshape(rows, -1)
    balanced = select(take, incoming.reshape(-1, part))
    tp = lax.axis_size("tp")
    width = gate_proj.shape[1]
    shipped = exchange(pack(balanced, 0, capacity))
    shipped_grad = exchange(after(packed_grad, shipped))

    def by_shard(partial):
        return rounded(partial).reshape(tp, -1, width)

    flat = shipped.reshape(-1, part)
    gate_part = by_shard(jnp.dot(flat, gate_proj, preferred_element_type=F32))
    flat = after(flat, gate_part)
    up_part = by_shard(jnp.dot(flat, up_proj, preferred_element_type=F32))
    marks_g, marks_u, marks_h, marks_o, marks_a, marks_b = [], [], [], [], [], []
    grad_parts = []

    def grad_part():
        arrived = after(shipped_grad, *marks_g[2]).reshape(-1, part)
        grad_parts.append(by_shard(dot_nt(arrived, down_proj)))
        return grad_parts[0]

    gate_pre = ring_scatter(gate_part, marks_g, True, grad_part)
    up_pre = ring_scatter(up_part, marks_u, False)
    hidden_grad = ring_scatter(grad_parts[0], marks_h, True)

    sigmoid_gate = jax.nn.sigmoid(gate_pre)
    hidden = (gate_pre * sigmoid_gate * up_pre).astype(BF)
    hidden = after(hidden, *marks_h[1])
    gate_pre, up_pre, sigmoid_gate = after((gate_pre, up_pre, sigmoid_gate), hidden)
    hidden = ring_gather(hidden, marks_o, False).reshape(-1, width)
    gate_grad = (
        hidden_grad * up_pre * sigmoid_gate * (1.0 + gate_pre * (1.0 - sigmoid_gate))
    ).astype(BF)
    up_grad = (hidden_grad * gate_pre * sigmoid_gate).astype(BF)
    inner = jnp.concatenate([gate_grad, up_grad], axis=1).reshape(-1, capacity, 2 * width)
    first = after(inner[:, :early], *marks_o[1]).reshape(-1, 2 * width)
    first = ring_gather(first, marks_a, True).reshape(-1, 2 * width)
    second = after(inner[:, early:], *marks_a[0]).reshape(-1, 2 * width)
    second = ring_gather(second, marks_b, False).reshape(-1, 2 * width)

    split = (members, -1, part)
    hidden = after(hidden, *marks_a[1])
    expert_out = jnp.dot(hidden, down_proj, preferred_element_type=F32).astype(BF)
    returned_out = exchange(expert_out.reshape(split))
    first = after(first, expert_out, *marks_b[1])
    first_grad = dot_nt(first, both_proj).astype(BF)
    second = after(second, first_grad)
    first_grad = exchange(after(first_grad, returned_out).reshape(split))
    second_grad = dot_nt(second, both_proj).astype(BF)
    second_grad = exchange(after(second_grad, first_grad).reshape(split))

    scale_high = lax.optimization_barrier(gate_scale.astype(BF))
    scale_low = (gate_scale - scale_high.astype(F32)).astype(BF)

    def weights(scale):
        per_expert = jnp.sum(jnp.where(chosen, scale.astype(F32).T[None], 0.0), axis=1)
        return jnp.where(hot, per_expert[:, None, :], 0.0).astype(BF).reshape(-1, rows)

    mix = jnp.concatenate([weights(scale_high), weights(scale_low)], axis=1)
    mix = mix.reshape(members, capacity, -1)

    def combine(mix, returned):
        both = lax.dot_general(
            mix.reshape(-1, mix.shape[2]),
            returned.reshape(-1, part),
            (((0,), (0,)), ((), ())),
            preferred_element_type=F32,
        )
        return both[:rows] + both[rows:]

    balanced_grad = combine(mix[:, :early], first_grad) + combine(mix[:, early:], second_grad)
    balanced_grad = balanced_grad.astype(BF)
    leaving = select_t(take, balanced_grad)
    arriving = exchange(leaving.reshape(members, per_peer, part))
    grad_rows = select_t(spread, arriving.reshape(-1, part))
    layer_out = combine(mix, returned_out).astype(BF)
    return (layer_out, grad_rows)


def solution(mesh):
    placed = (
        P("dp", "tp"),
        P("dp"),
        P("dp", None),
        P("dp", None),
        P("dp", "tp", None),
        P("dp", "tp", None),
        P("dp", None, "tp"),
        P("dp", "tp"),
    )
    return jax.shard_map(
        on_device,
        mesh=mesh,
        in_specs=placed,
        out_specs=(P("dp", "tp"), P("dp", "tp")),
        check_vma=False,
    )
```
